32 devices in a mesh: dp: 8 (over z, y), ctx: 4 (over x, core).
Axes of the slice: x: 2, y: 2, z: 4, core: 2. Of those that a mesh axis runs over, the one named last changes fastest.
Arguments:
- projected: bfloat16 [8, 512, 3, 4096], P('dp', 'ctx'), may hold values from -6 to 6
- short_taps: float32 [3, 3, 4096], P(None, None, 'ctx'), may hold values from -3 to 3
- long_filter: bfloat16 [512, 4096], P('dp', 'ctx'), may hold values from -1.1 to 1.1
- skip_gain: float32 [4096], P('ctx'), may hold values from -4 to 4
Outputs:
- mixed: bfloat16 [8, 512, 4096], P('dp', 'ctx')
The draws below stay inside these ranges and needn't reach their ends.
All inputs are finite; a program needn't handle non-finite values.
Results may differ from the reference program's by a relative error of at most 0.012.
Values may be sent and summed in bfloat16 or wider, within the bound.
A program may use at most 64 MiB of HBM per device.

```python
import math
import jax
import jax.numpy as jnp
from jax import lax

D = 4096
KSHORT = 3
SEQ_LEN = 512
SEQS = 8


def draw_long_filter(key, part):
    rate_key, tap_key = jax.random.split(jax.random.fold_in(key, 11))
    rate_low = 0.25 / SEQ_LEN
    rate_high = 1.0 / 30.0
    log_rate = jax.random.uniform(rate_key, (D,), jnp.float32, math.log(rate_low), math.log(rate_high))
    decay_rates = jnp.exp(log_rate)
    positions = jnp.arange(SEQ_LEN, dtype=jnp.float32)[:, None]
    envelope = jnp.exp(-decay_rates[None, :] * positions)
    scale_norm = jnp.sqrt(jnp.expm1(-2.0 * decay_rates) / jnp.expm1(-2.0 * decay_rates * SEQ_LEN))
    tap_noise = jnp.clip(jax.random.normal(tap_key, (SEQ_LEN, D), jnp.float32), -4.0, 4.0)
    return (tap_noise * envelope * scale_norm[None, :]).astype(jnp.bfloat16)


def shard_levels(stream_key, dims, pieces, least, high):
    factor_of = 1.0
    for dim, shards_of in pieces:
        draws = jax.random.uniform(jax.random.fold_in(jax.random.fold_in(stream_key, 6), dim), (shards_of,), jnp.float32, least / len(pieces), high / len(pieces))
        factor_of = factor_of * jnp.repeat(jnp.exp(draws), dims[dim] // shards_of).reshape((-1,) + (1,) * (len(dims) - 1 - dim))
    return factor_of


def gaussian(own_key, shape, spread, limit, pieces=(), kind=jnp.bfloat16):
    gain = shard_levels(own_key, shape, pieces, -0.22, 0.18) if pieces else 1.0
    array = jax.random.normal(own_key, shape, jnp.float32) * spread * gain
    return jnp.minimum(jnp.maximum(array, -limit), limit).astype(kind)


def setup_inputs(seed: int = 0) -> dict:
    keys = jax.random.split(jax.random.key(seed), 5)
    projected = gaussian(keys[0], (SEQS, SEQ_LEN, 3, D), 1.0, 6.0, ((0, 8), (1, 4)))
    short_taps = gaussian(keys[1], (KSHORT, 3, D), 0.6, 3.0, ((2, 4),), jnp.float32)
    long_filter = draw_long_filter(jax.random.fold_in(keys[4], 71), 0)
    skip_gain = gaussian(keys[3], (D,), 1.0, 4.0, ((0, 4),), jnp.float32)
    return {"projected": projected, "short_taps": short_taps, "long_filter": long_filter, "skip_gain": skip_gain}


def reference(projected, short_taps, long_filter, skip_gain):
    kernel_float = long_filter.astype(jnp.float32)
    fft_size = 2 * SEQ_LEN
    kernel_freq = jnp.fft.rfft(kernel_float, n=fft_size, axis=0)

    def per_sequence(sequence):
        widened = sequence.astype(jnp.float32)
        padded = jnp.pad(widened, ((KSHORT - 1, 0), (0, 0), (0, 0)))
        short_conv = jnp.zeros(widened.shape, jnp.float32)
        for tap_index in range(KSHORT):
            offset = KSHORT - 1 - tap_index
            short_conv = short_conv + short_taps[tap_index] * padded[offset:offset + SEQ_LEN]
        queries = short_conv[:, 0].astype(jnp.bfloat16)
        gated_rows = (short_conv[:, 1] * short_conv[:, 2]).astype(jnp.bfloat16)
        gated_float = gated_rows.astype(jnp.float32)
        spectrum = jnp.fft.rfft(gated_float, n=fft_size, axis=0) * kernel_freq
        long_part = jnp.fft.irfft(spectrum, n=fft_size, axis=0)[:SEQ_LEN]
        response = (long_part + skip_gain * gated_float).astype(jnp.bfloat16)
        return (queries.astype(jnp.float32) * response.astype(jnp.float32)).astype(jnp.bfloat16)

    return lax.map(per_sequence, projected)
```

```python
import math

import jax
import jax.numpy as jnp
import numpy as np
from jax import lax
from jax.sharding import PartitionSpec as P

RADIX = 64


HIGH = lax.Precision.HIGHEST


def causal_short(extended, taps, kernel_size):
    row_count = extended.shape[0] - (kernel_size - 1)
    widened = extended.astype(jnp.float32)
    summed = jnp.zeros((row_count,) + widened.shape[1:], jnp.float32)
    for tap_index in range(kernel_size):
        offset = kernel_size - 1 - tap_index
        summed = summed + taps[tap_index] * widened[offset : offset + row_count]
    return (summed[:, 0].astype(jnp.bfloat16), (summed[:, 1] * summed[:, 2]).astype(jnp.bfloat16))


def dft_tables(length, radix_size):
    outer_size = 2 * length // radix_size
    total_size = outer_size * radix_size
    outer_range = jnp.arange(outer_size, dtype=jnp.int32)
    inner_range = jnp.arange(radix_size, dtype=jnp.int32)
    angle_one = (
        2.0
        * math.pi
        / outer_size
        * (outer_range[:, None] * outer_range[None, :] % outer_size).astype(jnp.float32)
    )
    angle_twist = (
        2.0
        * math.pi
        / total_size
        * (outer_range[:, None] * inner_range[None, :] % total_size).astype(jnp.float32)
    )
    angle_two = (
        2.0
        * math.pi
        / radix_size
        * (inner_range[:, None] * inner_range[None, :] % radix_size).astype(jnp.float32)
    )
    twist_cos = jnp.cos(angle_twist)[:, :, None]
    twist_sin = jnp.sin(angle_twist)[:, :, None]
    return (
        jnp.cos(angle_one),
        jnp.sin(angle_one),
        twist_cos,
        twist_sin,
        jnp.cos(angle_two),
        jnp.sin(angle_two),
    )


def forward_dft(signal, tables, radix_size):
    cos_one, sin_one, twist_cos, twist_sin, cos_two, sin_two = tables
    outer_size = cos_one.shape[0]
    half_size = outer_size // 2
    block_width = signal.shape[1]
    shaped = signal.reshape(half_size, radix_size * block_width)
    first_re = jnp.dot(cos_one[:, :half_size], shaped, precision=HIGH).reshape(
        outer_size, radix_size, block_width
    )
    first_im = -jnp.dot(sin_one[:, :half_size], shaped, precision=HIGH).reshape(
        outer_size, radix_size, block_width
    )
    second_re = first_re * twist_cos + first_im * twist_sin
    second_im = first_im * twist_cos - first_re * twist_sin
    spec_re = jnp.einsum("amc,mb->abc", second_re, cos_two, precision=HIGH) + jnp.einsum(
        "amc,mb->abc", second_im, sin_two, precision=HIGH
    )
    spec_im = jnp.einsum("amc,mb->abc", second_im, cos_two, precision=HIGH) - jnp.einsum(
        "amc,mb->abc", second_re, sin_two, precision=HIGH
    )
    return (spec_re, spec_im)


def inverse_dft(spec_re, spec_im, tables, radix_size):
    cos_one, sin_one, twist_cos, twist_sin, cos_two, sin_two = tables
    outer_size = cos_one.shape[0]
    half_size = outer_size // 2
    block_width = spec_re.shape[2]
    back_re = jnp.einsum("abc,mb->amc", spec_re, cos_two, precision=HIGH) - jnp.einsum(
        "abc,mb->amc", spec_im, sin_two, precision=HIGH
    )
    back_im = jnp.einsum("abc,mb->amc", spec_re, sin_two, precision=HIGH) + jnp.einsum(
        "abc,mb->amc", spec_im, cos_two, precision=HIGH
    )
    turned_re = (back_re * twist_cos - back_im * twist_sin).reshape(
        outer_size, radix_size * block_width
    )
    turned_im = (back_re * twist_sin + back_im * twist_cos).reshape(
        outer_size, radix_size * block_width
    )
    result = jnp.dot(cos_one[:half_size], turned_re, precision=HIGH) - jnp.dot(
        sin_one[:half_size], turned_im, precision=HIGH
    )
    return result.reshape(half_size * radix_size, block_width) / (outer_size * radix_size)


def long_convolve_blocked(gated_slab, filter_slab):
    length, channels = gated_slab.shape
    block_width = min(128, channels)
    tables = dft_tables(length, RADIX)

    def one_block(block_index, output):
        offset = block_index * block_width
        signal = lax.dynamic_slice_in_dim(gated_slab, offset, block_width, 1).astype(jnp.float32)
        kernel_block = lax.dynamic_slice_in_dim(filter_slab, offset, block_width, 1).astype(
            jnp.float32
        )
        sig_re, sig_im = forward_dft(signal, tables, RADIX)
        ker_re, ker_im = forward_dft(kernel_block, tables, RADIX)
        prod_re = sig_re * ker_re - sig_im * ker_im
        prod_im = sig_re * ker_im + sig_im * ker_re
        result = inverse_dft(prod_re, prod_im, tables, RADIX)
        return lax.dynamic_update_slice_in_dim(output, result, offset, 1)

    return lax.fori_loop(
        0, channels // block_width, one_block, jnp.zeros((length, channels), jnp.float32)
    )


def long_convolve(gated_slab, filter_slab):
    length = gated_slab.shape[0]
    if length > 1024:
        return long_convolve_blocked(gated_slab, filter_slab)
    forward, backward = quarter_tables(length)
    sig = jnp.dot(forward, gated_slab, preferred_element_type=jnp.float32)
    ker = jnp.dot(forward, filter_slab, preferred_element_type=jnp.float32)
    sig_cos, sig_sin, ker_cos, ker_sin = sig[:length], sig[length:], ker[:length], ker[length:]
    prod = jnp.concatenate(
        [sig_cos * ker_cos - sig_sin * ker_sin, sig_cos * ker_sin + sig_sin * ker_cos]
    ).astype(jnp.bfloat16)
    return jnp.dot(backward, prod, preferred_element_type=jnp.float32)


def quarter_tables(length):
    steps = (4 * np.arange(length)[:, None] + 1) * np.arange(length)[None, :] % (4 * length)
    angles = steps * (2.0 * math.pi / (4 * length))
    table = np.concatenate([np.cos(angles), np.sin(angles)])
    return (jnp.asarray(table, jnp.bfloat16), jnp.asarray(table.T / length, jnp.bfloat16))


def make_response(gated_slab, filter_slab, skip_gain):
    long_part = long_convolve(gated_slab, filter_slab)
    return (long_part + skip_gain * gated_slab.astype(jnp.float32)).astype(jnp.bfloat16)


def combine_rows(query_part, response_part):
    return (query_part.astype(jnp.float32) * response_part.astype(jnp.float32)).astype(jnp.bfloat16)


def on_device(projected, short_taps, long_filter, skip_gain):
    kernel_size = short_taps.shape[0]
    ctx_size = lax.axis_size("ctx")
    rows = projected[0]
    filter_slab = lax.all_gather(long_filter, "dp", axis=0, tiled=True)
    all_taps = lax.all_gather(short_taps, "ctx", axis=2, tiled=True)
    halo = lax.ppermute(
        rows[-(kernel_size - 1) :], "ctx", [(i, i + 1) for i in range(ctx_size - 1)]
    )
    queries, gated = causal_short(jnp.concatenate([halo, rows]), all_taps, kernel_size)
    gated_slab = lax.all_to_all(gated, "ctx", split_axis=1, concat_axis=0, tiled=True)
    response_slab = make_response(gated_slab, filter_slab, skip_gain)
    response = lax.all_to_all(response_slab, "ctx", split_axis=0, concat_axis=1, tiled=True)
    return combine_rows(queries, response)[None]


def solution(mesh):
    return jax.shard_map(
        on_device,
        mesh=mesh,
        in_specs=(P("dp", "ctx", None, None), P(None, None, "ctx"), P("dp", "ctx"), P("ctx")),
        out_specs=P("dp", "ctx", None),
        check_vma=False,
    )
```

```python
import functools
import math

import jax
import jax.numpy as jnp
import numpy as np
from jax import lax
from jax.experimental import pallas as pl
from jax.experimental.pallas import tpu as pltpu
from jax.sharding import PartitionSpec as P

RADIX = 64


HIGH = lax.Precision.HIGHEST


def causal_short(extended, taps, kernel_size):
    row_count = extended.shape[0] - (kernel_size - 1)
    widened = extended.astype(jnp.float32)
    summed = jnp.zeros((row_count,) + widened.shape[1:], jnp.float32)
    for tap_index in range(kernel_size):
        offset = kernel_size - 1 - tap_index
        summed = summed + taps[tap_index] * widened[offset : offset + row_count]
    return (summed[:, 0].astype(jnp.bfloat16), (summed[:, 1] * summed[:, 2]).astype(jnp.bfloat16))


def dft_tables(length, radix_size):
    outer_size = 2 * length // radix_size
    total_size = outer_size * radix_size
    outer_range = jnp.arange(outer_size, dtype=jnp.int32)
    inner_range = jnp.arange(radix_size, dtype=jnp.int32)
    angle_one = (
        2.0
        * math.pi
        / outer_size
        * (outer_range[:, None] * outer_range[None, :] % outer_size).astype(jnp.float32)
    )
    angle_twist = (
        2.0
        * math.pi
        / total_size
        * (outer_range[:, None] * inner_range[None, :] % total_size).astype(jnp.float32)
    )
    angle_two = (
        2.0
        * math.pi
        / radix_size
        * (inner_range[:, None] * inner_range[None, :] % radix_size).astype(jnp.float32)
    )
    twist_cos = jnp.cos(angle_twist)[:, :, None]
    twist_sin = jnp.sin(angle_twist)[:, :, None]
    return (
        jnp.cos(angle_one),
        jnp.sin(angle_one),
        twist_cos,
        twist_sin,
        jnp.cos(angle_two),
        jnp.sin(angle_two),
    )


def forward_dft(signal, tables, radix_size):
    cos_one, sin_one, twist_cos, twist_sin, cos_two, sin_two = tables
    outer_size = cos_one.shape[0]
    half_size = outer_size // 2
    block_width = signal.shape[1]
    shaped = signal.reshape(half_size, radix_size * block_width)
    first_re = jnp.dot(cos_one[:, :half_size], shaped, precision=HIGH).reshape(
        outer_size, radix_size, block_width
    )
    first_im = -jnp.dot(sin_one[:, :half_size], shaped, precision=HIGH).reshape(
        outer_size, radix_size, block_width
    )
    second_re = first_re * twist_cos + first_im * twist_sin
    second_im = first_im * twist_cos - first_re * twist_sin
    spec_re = jnp.einsum("amc,mb->abc", second_re, cos_two, precision=HIGH) + jnp.einsum(
        "amc,mb->abc", second_im, sin_two, precision=HIGH
    )
    spec_im = jnp.einsum("amc,mb->abc", second_im, cos_two, precision=HIGH) - jnp.einsum(
        "amc,mb->abc", second_re, sin_two, precision=HIGH
    )
    return (spec_re, spec_im)


def inverse_dft(spec_re, spec_im, tables, radix_size):
    cos_one, sin_one, twist_cos, twist_sin, cos_two, sin_two = tables
    outer_size = cos_one.shape[0]
    half_size = outer_size // 2
    block_width = spec_re.shape[2]
    back_re = jnp.einsum("abc,mb->amc", spec_re, cos_two, precision=HIGH) - jnp.einsum(
        "abc,mb->amc", spec_im, sin_two, precision=HIGH
    )
    back_im = jnp.einsum("abc,mb->amc", spec_re, sin_two, precision=HIGH) + jnp.einsum(
        "abc,mb->amc", spec_im, cos_two, precision=HIGH
    )
    turned_re = (back_re * twist_cos - back_im * twist_sin).reshape(
        outer_size, radix_size * block_width
    )
    turned_im = (back_re * twist_sin + back_im * twist_cos).reshape(
        outer_size, radix_size * block_width
    )
    result = jnp.dot(cos_one[:half_size], turned_re, precision=HIGH) - jnp.dot(
        sin_one[:half_size], turned_im, precision=HIGH
    )
    return result.reshape(half_size * radix_size, block_width) / (outer_size * radix_size)


def long_convolve_blocked(gated_slab, filter_slab):
    length, channels = gated_slab.shape
    block_width = min(128, channels)
    tables = dft_tables(length, RADIX)

    def one_block(block_index, output):
        offset = block_index * block_width
        signal = lax.dynamic_slice_in_dim(gated_slab, offset, block_width, 1).astype(jnp.float32)
        kernel_block = lax.dynamic_slice_in_dim(filter_slab, offset, block_width, 1).astype(
            jnp.float32
        )
        sig_re, sig_im = forward_dft(signal, tables, RADIX)
        ker_re, ker_im = forward_dft(kernel_block, tables, RADIX)
        prod_re = sig_re * ker_re - sig_im * ker_im
        prod_im = sig_re * ker_im + sig_im * ker_re
        result = inverse_dft(prod_re, prod_im, tables, RADIX)
        return lax.dynamic_update_slice_in_dim(output, result, offset, 1)

    return lax.fori_loop(
        0, channels // block_width, one_block, jnp.zeros((length, channels), jnp.float32)
    )


def long_convolve(gated_slab, filter_slab):
    length = gated_slab.shape[0]
    if length > 1024:
        return long_convolve_blocked(gated_slab, filter_slab)
    forward, backward = quarter_tables(length)
    sig = jnp.dot(forward, gated_slab, preferred_element_type=jnp.float32)
    ker = jnp.dot(forward, filter_slab, preferred_element_type=jnp.float32)
    sig_cos, sig_sin, ker_cos, ker_sin = sig[:length], sig[length:], ker[:length], ker[length:]
    prod = jnp.concatenate(
        [sig_cos * ker_cos - sig_sin * ker_sin, sig_cos * ker_sin + sig_sin * ker_cos]
    ).astype(jnp.bfloat16)
    return jnp.dot(backward, prod, preferred_element_type=jnp.float32)


def quarter_tables(length):
    steps = (4 * np.arange(length)[:, None] + 1) * np.arange(length)[None, :] % (4 * length)
    angles = steps * (2.0 * math.pi / (4 * length))
    table = np.concatenate([np.cos(angles), np.sin(angles)])
    return (jnp.asarray(table, jnp.bfloat16), jnp.asarray(table.T / length, jnp.bfloat16))


def make_response(gated_slab, filter_slab, skip_gain):
    long_part = long_convolve(gated_slab, filter_slab)
    return (long_part + skip_gain * gated_slab.astype(jnp.float32)).astype(jnp.bfloat16)


def combine_rows(query_part, response_part):
    return (query_part.astype(jnp.float32) * response_part.astype(jnp.float32)).astype(jnp.bfloat16)


def on_device_large(projected, short_taps, long_filter, skip_gain):
    kernel_size = short_taps.shape[0]
    ctx_size = lax.axis_size("ctx")
    rows = projected[0]
    filter_slab = lax.all_gather(long_filter, "dp", axis=0, tiled=True)
    all_taps = lax.all_gather(short_taps, "ctx", axis=2, tiled=True)
    halo = lax.ppermute(
        rows[-(kernel_size - 1) :], "ctx", [(i, i + 1) for i in range(ctx_size - 1)]
    )
    queries, gated = causal_short(jnp.concatenate([halo, rows]), all_taps, kernel_size)
    gated_slab = lax.all_to_all(gated, "ctx", split_axis=1, concat_axis=0, tiled=True)
    response_slab = make_response(gated_slab, filter_slab, skip_gain)
    response = lax.all_to_all(response_slab, "ctx", split_axis=0, concat_axis=1, tiled=True)
    return combine_rows(queries, response)[None]


CHUNK = 256
MESH = pl.DeviceIdType.MESH


def ctx_offsets(ctx_size):
    pairs = [(a, b) for a in range(1, ctx_size // 2) for b in range(2)]
    return pairs + [(0, 1)]


def ctx_peer(me, offset, ctx_size, sign):
    half = ctx_size // 2
    chip = lax.rem(me // 2 + (half + sign * offset[0]) % half, half)
    core = lax.rem(lax.rem(me, 2) + offset[1], 2)
    return chip * 2 + core


def mixer_kernel(
    ctx_size,
    dp_size,
    x_hbm,
    taps_ref,
    filter_ref,
    skip_ref,
    forward_hbm,
    backward_hbm,
    out_ref,
    x_ref,
    forward_ref,
    backward_ref,
    taps_all,
    halo_out,
    halo_in,
    gated_out,
    gated_slab,
    filter_slab,
    filter_spec,
    prod_ref,
    response_slab,
    response_in,
    queries,
    local_sem,
    taps_send,
    taps_recv,
    halo_send,
    halo_recv,
    zfil_send,
    zfil_recv,
    yfil_send,
    yfil_recv,
    gated_send,
    gated_recv,
    resp_send,
    resp_recv,
):
    kernel_size = taps_ref.shape[0]
    channels = taps_ref.shape[2]
    rows = x_ref.shape[1]
    length = rows * ctx_size
    chunks = channels // CHUNK
    fil_rows = filter_ref.shape[0]
    zsize = dp_size // 2
    me = lax.axis_index("ctx")
    dp = lax.axis_index("dp")
    zpos, ypos = dp // 2, lax.rem(dp, 2)
    offsets = ctx_offsets(ctx_size)
    dests = [ctx_peer(me, o, ctx_size, 1) for o in offsets]
    sources = [ctx_peer(me, o, ctx_size, -1) for o in offsets]
    following = lax.rem(me + 1, ctx_size)
    zpeers = [lax.rem(zpos + k, zsize) * 2 + ypos for k in range(1, zsize)]
    zsources = [lax.rem(zpos + zsize - k, zsize) * 2 + ypos for k in range(1, zsize)]
    ypeer = zpos * 2 + (1 - ypos)

    x_copy = pltpu.make_async_copy(x_hbm, x_ref, local_sem.at[0])
    x_copy.start()
    forward_copy = pltpu.make_async_copy(forward_hbm, forward_ref, local_sem.at[1])
    forward_copy.start()
    backward_copy = pltpu.make_async_copy(backward_hbm, backward_ref, local_sem.at[2])
    backward_copy.start()

    barrier = pltpu.get_barrier_semaphore()
    for dest in dests:
        pl.semaphore_signal(barrier, inc=1, device_id={"ctx": dest}, device_id_type=MESH)
    for peer in zpeers + [ypeer]:
        pl.semaphore_signal(barrier, inc=1, device_id={"dp": peer}, device_id_type=MESH)
    pl.semaphore_wait(barrier, len(dests) + len(zpeers) + 1)

    def taps_copy(i, slot):
        return pltpu.make_async_remote_copy(
            src_ref=taps_ref,
            dst_ref=taps_all.at[slot],
            send_sem=taps_send.at[i],
            recv_sem=taps_recv.at[i],
            device_id={"ctx": dests[i]},
            device_id_type=MESH,
        )

    def filter_block(block):
        return filter_slab.at[pl.ds(pl.multiple_of(block * fil_rows, fil_rows), fil_rows), :]

    def zfil_copy(k, block):
        return pltpu.make_async_remote_copy(
            src_ref=filter_ref,
            dst_ref=filter_block(block),
            send_sem=zfil_send.at[k],
            recv_sem=zfil_recv.at[k],
            device_id={"dp": zpeers[k]},
            device_id_type=MESH,
        )

    def yfil_copy(k, source, block):
        return pltpu.make_async_remote_copy(
            src_ref=source,
            dst_ref=filter_block(block),
            send_sem=yfil_send.at[k],
            recv_sem=yfil_recv.at[k],
            device_id={"dp": ypeer},
            device_id_type=MESH,
        )

    for i in range(len(offsets)):
        taps_copy(i, me).start()
    x_copy.wait()
    halo_out[...] = x_ref[:, rows - (kernel_size - 1) :, :]
    halo_copy = pltpu.make_async_remote_copy(
        src_ref=halo_out,
        dst_ref=halo_in,
        send_sem=halo_send,
        recv_sem=halo_recv,
        device_id={"ctx": following},
        device_id_type=MESH,
    )
    halo_copy.start()
    for k in range(zsize - 1):
        zfil_copy(k, dp).start()
    yfil_copy(0, filter_ref, dp).start()
    taps_all[me] = taps_ref[...]
    filter_block(dp)[...] = filter_ref[...]
    for i in range(len(offsets)):
        taps_copy(i, sources[i]).wait_recv()
    halo_copy.wait_recv()

    row_index = lax.broadcasted_iota(jnp.int32, (rows, CHUNK), 0)

    def short_filter(stream, owner, chunk):
        columns = pl.ds(pl.multiple_of(owner * channels + chunk * CHUNK, CHUNK), CHUNK)
        taps_columns = pl.ds(pl.multiple_of(chunk * CHUNK, CHUNK), CHUNK)
        values = x_ref[stream, :, columns].astype(jnp.float32)
        edge = halo_in[stream, :, columns].astype(jnp.float32)
        edge = jnp.where(me > 0, edge, jnp.zeros_like(edge))
        total = taps_all[owner, 0, stream : stream + 1, taps_columns] * values
        for tap in range(1, kernel_size):
            moved = pltpu.roll(values, tap, 0)
            for row in range(tap):
                at = kernel_size - 1 + row - tap
                moved = jnp.where(row_index == row, edge[at : at + 1], moved)
            total = total + taps_all[owner, tap, stream : stream + 1, taps_columns] * moved
        return total

    def gated_rows(owner, chunk):
        return (short_filter(1, owner, chunk) * short_filter(2, owner, chunk)).astype(jnp.bfloat16)

    def position_rows(owner):
        return pl.ds(pl.multiple_of(owner * rows, rows), rows)

    def gated_copy(i, chunk, owner):
        return pltpu.make_async_remote_copy(
            src_ref=gated_out.at[i, chunk],
            dst_ref=gated_slab.at[chunk, position_rows(owner), :],
            send_sem=gated_send.at[i, chunk],
            recv_sem=gated_recv.at[i, chunk],
            device_id={"ctx": dests[i]},
            device_id_type=MESH,
        )

    def response_copy(i, chunk):
        return pltpu.make_async_remote_copy(
            src_ref=response_slab.at[chunk, position_rows(dests[i]), :],
            dst_ref=response_in.at[i, chunk],
            send_sem=resp_send.at[i, chunk],
            recv_sem=resp_recv.at[i, chunk],
            device_id={"ctx": dests[i]},
            device_id_type=MESH,
        )

    def push_gated(chunk, carry):
        for i in range(len(offsets)):
            gated_out[i, chunk] = gated_rows(dests[i], chunk)
            gated_copy(i, chunk, me).start()
        gated_slab[chunk, position_rows(me), :] = gated_rows(me, chunk)
        return carry

    lax.fori_loop(0, chunks, push_gated, 0)

    def make_queries(step, carry):
        owner, chunk = step // chunks, lax.rem(step, chunks)
        queries[owner, chunk] = short_filter(0, owner, chunk).astype(jnp.bfloat16)
        return carry

    for k in range(zsize - 1):
        zfil_copy(k, zsources[k]).wait_recv()
        yfil_copy(k + 1, filter_block(zsources[k]), zsources[k]).start()
    lax.fori_loop(0, chunks * ctx_size, make_queries, 0)
    forward_copy.wait()
    yfil_copy(0, filter_ref, ypeer).wait_recv()
    for k in range(zsize - 1):
        block = zsources[k] - ypos + (1 - ypos)
        yfil_copy(k + 1, filter_ref, block).wait_recv()

    def filter_spectrum(chunk, carry):
        columns = pl.ds(pl.multiple_of(chunk * CHUNK, CHUNK), CHUNK)
        filter_spec[chunk] = jnp.dot(
            forward_ref[...], filter_slab[:, columns], preferred_element_type=jnp.float32
        )
        return carry

    lax.fori_loop(0, chunks, filter_spectrum, 0)
    backward_copy.wait()

    def convolve(chunk, carry):
        for i in range(len(offsets)):
            gated_copy(i, chunk, sources[i]).wait_recv()
        gated = gated_slab[chunk]
        sig_cos = jnp.dot(forward_ref[:length], gated, preferred_element_type=jnp.float32)
        sig_sin = jnp.dot(forward_ref[length:], gated, preferred_element_type=jnp.float32)
        ker_cos, ker_sin = filter_spec[chunk, :length], filter_spec[chunk, length:]
        prod_ref[:length] = (sig_cos * ker_cos - sig_sin * ker_sin).astype(jnp.bfloat16)
        prod_ref[length:] = (sig_cos * ker_sin + sig_sin * ker_cos).astype(jnp.bfloat16)
        long_part = jnp.dot(backward_ref[...], prod_ref[...], preferred_element_type=jnp.float32)
        columns = pl.ds(pl.multiple_of(chunk * CHUNK, CHUNK), CHUNK)
        direct = skip_ref[:, columns] * gated.astype(jnp.float32)
        response_slab[chunk] = (long_part + direct).astype(jnp.bfloat16)
        for i in range(len(offsets)):
            response_copy(i, chunk).start()
        mix_into(me, chunk, response_slab[chunk, position_rows(me), :])
        return carry

    def mix_into(owner, chunk, response):
        columns = pl.ds(pl.multiple_of(owner * channels + chunk * CHUNK, CHUNK), CHUNK)
        mixed = queries[owner, chunk].astype(jnp.float32) * response.astype(jnp.float32)
        out_ref[:, columns] = mixed.astype(jnp.bfloat16)

    lax.fori_loop(0, chunks, convolve, 0)

    def finish(chunk, carry):
        for i in reversed(range(len(offsets))):
            response_copy(i, chunk).wait_recv()
            mix_into(sources[i], chunk, response_in[i, chunk])
        return carry

    lax.fori_loop(0, chunks, finish, 0)

    def drain(chunk, carry):
        for i in range(len(offsets)):
            gated_copy(i, chunk, me).wait_send()
            response_copy(i, chunk).wait_send()
        return carry

    lax.fori_loop(0, chunks, drain, 0)
    for i in range(len(offsets)):
        taps_copy(i, me).wait_send()
    halo_copy.wait_send()
    for k in range(zsize - 1):
        zfil_copy(k, dp).wait_send()
    yfil_copy(0, filter_ref, dp).wait_send()
    for k in range(zsize - 1):
        yfil_copy(k + 1, filter_block(zsources[k]), zsources[k]).wait_send()


def on_device(projected, short_taps, long_filter, skip_gain):
    ctx_size, dp_size = lax.axis_size("ctx"), lax.axis_size("dp")
    kernel_size, streams, channels = short_taps.shape
    rows, width = projected.shape[1], projected.shape[3]
    length = rows * ctx_size
    regular = ctx_size % 2 == 0 and dp_size % 2 == 0 and channels % CHUNK == 0
    if length > 1024 or not regular:
        return on_device_large(projected, short_taps, long_filter, skip_gain)
    forward, backward = quarter_tables(length)
    chunks = channels // CHUNK
    peers = ctx_size - 1
    zsize = dp_size // 2
    any_spec = pl.BlockSpec(memory_space=pl.ANY)
    vmem_spec = pl.BlockSpec(memory_space=pltpu.VMEM)
    dma = pltpu.SemaphoreType.DMA
    mixed = pl.pallas_call(
        functools.partial(mixer_kernel, ctx_size, dp_size),
        out_shape=jax.ShapeDtypeStruct((rows, width), jnp.bfloat16),
        in_specs=[any_spec, vmem_spec, vmem_spec, vmem_spec, any_spec, any_spec],
        out_specs=vmem_spec,
        scratch_shapes=[
            pltpu.VMEM((streams, rows, width), jnp.bfloat16),
            pltpu.VMEM(forward.shape, jnp.bfloat16),
            pltpu.VMEM(backward.shape, jnp.bfloat16),
            pltpu.VMEM((ctx_size, kernel_size, streams, channels), jnp.float32),
            pltpu.VMEM((streams, kernel_size - 1, width), jnp.bfloat16),
            pltpu.VMEM((streams, kernel_size - 1, width), jnp.bfloat16),
            pltpu.VMEM((peers, chunks, rows, CHUNK), jnp.bfloat16),
            pltpu.VMEM((chunks, length, CHUNK), jnp.bfloat16),
            pltpu.VMEM((length, channels), jnp.bfloat16),
            pltpu.VMEM((chunks, 2 * length, CHUNK), jnp.float32),
            pltpu.VMEM((2 * length, CHUNK), jnp.bfloat16),
            pltpu.VMEM((chunks, length, CHUNK), jnp.bfloat16),
            pltpu.VMEM((peers, chunks, rows, CHUNK), jnp.bfloat16),
            pltpu.VMEM((ctx_size, chunks, rows, CHUNK), jnp.bfloat16),
            dma((3,)),
            dma((peers,)),
            dma((peers,)),
            dma,
            dma,
            dma((zsize - 1,)),
            dma((zsize - 1,)),
            dma((zsize,)),
            dma((zsize,)),
            dma((peers, chunks)),
            dma((peers, chunks)),
            dma((peers, chunks)),
            dma((peers, chunks)),
        ],
        compiler_params=pltpu.CompilerParams(
            collective_id=0, has_side_effects=True, vmem_limit_bytes=48 * 2**20
        ),
    )(
        projected[0].transpose(1, 0, 2),
        short_taps,
        long_filter,
        skip_gain[None],
        forward,
        backward,
    )
    return mixed[None]


def solution(mesh):
    return jax.shard_map(
        on_device,
        mesh=mesh,
        in_specs=(P("dp", "ctx", None, None), P(None, None, "ctx"), P("dp", "ctx"), P("ctx")),
        out_specs=P("dp", "ctx", None),
        check_vma=False,
    )
```

```python
import functools
import math

import jax
import jax.numpy as jnp
import numpy as np
from jax import lax
from jax.experimental import pallas as pl
from jax.experimental.pallas import tpu as pltpu
from jax.sharding import PartitionSpec as P

RADIX = 64


HIGH = lax.Precision.HIGHEST


def causal_short(extended, taps, kernel_size):
    row_count = extended.shape[0] - (kernel_size - 1)
    widened = extended.astype(jnp.float32)
    summed = jnp.zeros((row_count,) + widened.shape[1:], jnp.float32)
    for tap_index in range(kernel_size):
        offset = kernel_size - 1 - tap_index
        summed = summed + taps[tap_index] * widened[offset : offset + row_count]
    return (summed[:, 0].astype(jnp.bfloat16), (summed[:, 1] * summed[:, 2]).astype(jnp.bfloat16))


def dft_tables(length, radix_size):
    outer_size = 2 * length // radix_size
    total_size = outer_size * radix_size
    outer_range = jnp.arange(outer_size, dtype=jnp.int32)
    inner_range = jnp.arange(radix_size, dtype=jnp.int32)
    angle_one = (
        2.0
        * math.pi
        / outer_size
        * (outer_range[:, None] * outer_range[None, :] % outer_size).astype(jnp.float32)
    )
    angle_twist = (
        2.0
        * math.pi
        / total_size
        * (outer_range[:, None] * inner_range[None, :] % total_size).astype(jnp.float32)
    )
    angle_two = (
        2.0
        * math.pi
        / radix_size
        * (inner_range[:, None] * inner_range[None, :] % radix_size).astype(jnp.float32)
    )
    twist_cos = jnp.cos(angle_twist)[:, :, None]
    twist_sin = jnp.sin(angle_twist)[:, :, None]
    return (
        jnp.cos(angle_one),
        jnp.sin(angle_one),
        twist_cos,
        twist_sin,
        jnp.cos(angle_two),
        jnp.sin(angle_two),
    )


def forward_dft(signal, tables, radix_size):
    cos_one, sin_one, twist_cos, twist_sin, cos_two, sin_two = tables
    outer_size = cos_one.shape[0]
    half_size = outer_size // 2
    block_width = signal.shape[1]
    shaped = signal.reshape(half_size, radix_size * block_width)
    first_re = jnp.dot(cos_one[:, :half_size], shaped, precision=HIGH).reshape(
        outer_size, radix_size, block_width
    )
    first_im = -jnp.dot(sin_one[:, :half_size], shaped, precision=HIGH).reshape(
        outer_size, radix_size, block_width
    )
    second_re = first_re * twist_cos + first_im * twist_sin
    second_im = first_im * twist_cos - first_re * twist_sin
    spec_re = jnp.einsum("amc,mb->abc", second_re, cos_two, precision=HIGH) + jnp.einsum(
        "amc,mb->abc", second_im, sin_two, precision=HIGH
    )
    spec_im = jnp.einsum("amc,mb->abc", second_im, cos_two, precision=HIGH) - jnp.einsum(
        "amc,mb->abc", second_re, sin_two, precision=HIGH
    )
    return (spec_re, spec_im)


def inverse_dft(spec_re, spec_im, tables, radix_size):
    cos_one, sin_one, twist_cos, twist_sin, cos_two, sin_two = tables
    outer_size = cos_one.shape[0]
    half_size = outer_size // 2
    block_width = spec_re.shape[2]
    back_re = jnp.einsum("abc,mb->amc", spec_re, cos_two, precision=HIGH) - jnp.einsum(
        "abc,mb->amc", spec_im, sin_two, precision=HIGH
    )
    back_im = jnp.einsum("abc,mb->amc", spec_re, sin_two, precision=HIGH) + jnp.einsum(
        "abc,mb->amc", spec_im, cos_two, precision=HIGH
    )
    turned_re = (back_re * twist_cos - back_im * twist_sin).reshape(
        outer_size, radix_size * block_width
    )
    turned_im = (back_re * twist_sin + back_im * twist_cos).reshape(
        outer_size, radix_size * block_width
    )
    result = jnp.dot(cos_one[:half_size], turned_re, precision=HIGH) - jnp.dot(
        sin_one[:half_size], turned_im, precision=HIGH
    )
    return result.reshape(half_size * radix_size, block_width) / (outer_size * radix_size)


def long_convolve_blocked(gated_slab, filter_slab):
    length, channels = gated_slab.shape
    block_width = min(128, channels)
    tables = dft_tables(length, RADIX)

    def one_block(block_index, output):
        offset = block_index * block_width
        signal = lax.dynamic_slice_in_dim(gated_slab, offset, block_width, 1).astype(jnp.float32)
        kernel_block = lax.dynamic_slice_in_dim(filter_slab, offset, block_width, 1).astype(
            jnp.float32
        )
        sig_re, sig_im = forward_dft(signal, tables, RADIX)
        ker_re, ker_im = forward_dft(kernel_block, tables, RADIX)
        prod_re = sig_re * ker_re - sig_im * ker_im
        prod_im = sig_re * ker_im + sig_im * ker_re
        result = inverse_dft(prod_re, prod_im, tables, RADIX)
        return lax.dynamic_update_slice_in_dim(output, result, offset, 1)

    return lax.fori_loop(
        0, channels // block_width, one_block, jnp.zeros((length, channels), jnp.float32)
    )


def long_convolve(gated_slab, filter_slab):
    length = gated_slab.shape[0]
    if length > 1024:
        return long_convolve_blocked(gated_slab, filter_slab)
    forward, backward = quarter_tables(length)
    sig = jnp.dot(forward, gated_slab, preferred_element_type=jnp.float32)
    ker = jnp.dot(forward, filter_slab, preferred_element_type=jnp.float32)
    sig_cos, sig_sin, ker_cos, ker_sin = sig[:length], sig[length:], ker[:length], ker[length:]
    prod = jnp.concatenate(
        [sig_cos * ker_cos - sig_sin * ker_sin, sig_cos * ker_sin + sig_sin * ker_cos]
    ).astype(jnp.bfloat16)
    return jnp.dot(backward, prod, preferred_element_type=jnp.float32)


def quarter_tables(length):
    steps = (4 * np.arange(length)[:, None] + 1) * np.arange(length)[None, :] % (4 * length)
    angles = steps * (2.0 * math.pi / (4 * length))
    table = np.concatenate([np.cos(angles), np.sin(angles)])
    return (jnp.asarray(table, jnp.bfloat16), jnp.asarray(table.T / length, jnp.bfloat16))


def make_response(gated_slab, filter_slab, skip_gain):
    long_part = long_convolve(gated_slab, filter_slab)
    return (long_part + skip_gain * gated_slab.astype(jnp.float32)).astype(jnp.bfloat16)


def combine_rows(query_part, response_part):
    return (query_part.astype(jnp.float32) * response_part.astype(jnp.float32)).astype(jnp.bfloat16)


def on_device_large(projected, short_taps, long_filter, skip_gain):
    kernel_size = short_taps.shape[0]
    ctx_size = lax.axis_size("ctx")
    rows = projected[0]
    filter_slab = lax.all_gather(long_filter, "dp", axis=0, tiled=True)
    all_taps = lax.all_gather(short_taps, "ctx", axis=2, tiled=True)
    halo = lax.ppermute(
        rows[-(kernel_size - 1) :], "ctx", [(i, i + 1) for i in range(ctx_size - 1)]
    )
    queries, gated = causal_short(jnp.concatenate([halo, rows]), all_taps, kernel_size)
    gated_slab = lax.all_to_all(gated, "ctx", split_axis=1, concat_axis=0, tiled=True)
    response_slab = make_response(gated_slab, filter_slab, skip_gain)
    response = lax.all_to_all(response_slab, "ctx", split_axis=0, concat_axis=1, tiled=True)
    return combine_rows(queries, response)[None]


CHUNK = 256
MESH = pl.DeviceIdType.MESH


def ctx_offsets(ctx_size):
    pairs = [(a, b) for a in range(1, ctx_size // 2) for b in range(2)]
    return pairs + [(0, 1)]


def ctx_peer(me, offset, ctx_size, sign):
    half = ctx_size // 2
    chip = lax.rem(me // 2 + (half + sign * offset[0]) % half, half)
    core = lax.rem(lax.rem(me, 2) + offset[1], 2)
    return chip * 2 + core


def mixer_kernel(
    ctx_size,
    dp_size,
    x_hbm,
    taps_ref,
    filter_ref,
    skip_hbm,
    forward_hbm,
    backward_hbm,
    out_hbm,
    x_ref,
    skip_ref,
    forward_ref,
    backward_ref,
    taps_all,
    halo_out,
    halo_in,
    gated_out,
    gated_slab,
    filter_slab,
    filter_spec,
    prod_ref,
    response_slab,
    response_in,
    queries,
    local_sem,
    taps_send,
    taps_recv,
    halo_send,
    halo_recv,
    zfil_send,
    zfil_recv,
    yfil_send,
    yfil_recv,
    gated_send,
    gated_recv,
    resp_send,
    resp_recv,
    out_sem,
    filter_sem,
):
    kernel_size = taps_ref.shape[0]
    channels = taps_ref.shape[2]
    rows = x_ref.shape[1]
    length = rows * ctx_size
    chunks = channels // CHUNK
    fil_rows = filter_ref.shape[0]
    zsize = dp_size // 2
    me = lax.axis_index("ctx")
    dp = lax.axis_index("dp")
    zpos, ypos = dp // 2, lax.rem(dp, 2)
    offsets = ctx_offsets(ctx_size)
    dests = [ctx_peer(me, o, ctx_size, 1) for o in offsets]
    sources = [ctx_peer(me, o, ctx_size, -1) for o in offsets]
    following = lax.rem(me + 1, ctx_size)
    ypeer = zpos * 2 + (1 - ypos)

    def filter_block(block, chunk):
        return filter_slab.at[
            chunk, pl.ds(pl.multiple_of(block * fil_rows, fil_rows), fil_rows), :
        ]

    def own_filter(chunk):
        return filter_ref.at[:, pl.ds(pl.multiple_of(chunk * CHUNK, CHUNK), CHUNK)]

    def own_filter_copy(chunk):
        return pltpu.make_async_copy(
            own_filter(chunk), filter_block(dp, chunk), filter_sem.at[chunk]
        )

    x_copy = pltpu.make_async_copy(x_hbm, x_ref, local_sem.at[0])
    x_copy.start()
    forward_copy = pltpu.make_async_copy(forward_hbm, forward_ref, local_sem.at[1])
    forward_copy.start()
    backward_copy = pltpu.make_async_copy(backward_hbm, backward_ref, local_sem.at[2])
    backward_copy.start()
    skip_copy = pltpu.make_async_copy(skip_hbm, skip_ref, local_sem.at[3])
    skip_copy.start()
    own_taps_copy = pltpu.make_async_copy(taps_ref, taps_all.at[me], local_sem.at[4])
    own_taps_copy.start()
    for chunk in range(chunks):
        own_filter_copy(chunk).start()

    barrier = pltpu.get_barrier_semaphore()
    for dest in dests:
        pl.semaphore_signal(barrier, inc=1, device_id={"ctx": dest}, device_id_type=MESH)
    pl.semaphore_signal(barrier, inc=1, device_id={"dp": ypeer}, device_id_type=MESH)

    for turn in (1, zsize - 1):
        side_peer = lax.rem(zpos + turn, zsize) * 2 + ypos
        pl.semaphore_signal(barrier, inc=1, device_id={"dp": side_peer}, device_id_type=MESH)
    pl.semaphore_wait(barrier, len(dests) + 3)

    def taps_copy(i, source, slot):
        return pltpu.make_async_remote_copy(
            src_ref=source,
            dst_ref=taps_all.at[slot],
            send_sem=taps_send.at[i],
            recv_sem=taps_recv.at[i],
            device_id={"ctx": dests[i] if offsets[i][1] == 0 else dests[-1]},
            device_id_type=MESH,
        )

    def zfil_copy(side, step, source, block, chunk):
        return pltpu.make_async_remote_copy(
            src_ref=source,
            dst_ref=filter_block(block, chunk),
            send_sem=zfil_send.at[side, step, chunk],
            recv_sem=zfil_recv.at[side, step, chunk],
            device_id={"dp": dp + 2 - 4 * side},
            device_id_type=MESH,
        )

    def yfil_copy(side, step, source, block, chunk):
        return pltpu.make_async_remote_copy(
            src_ref=source,
            dst_ref=filter_block(block, chunk),
            send_sem=yfil_send.at[side, step, chunk],
            recv_sem=yfil_recv.at[side, step, chunk],
            device_id={"dp": ypeer},
            device_id_type=MESH,
        )

    has_next = (zpos < zsize - 1, zpos > 0)

    def origin(side, step):
        return zpos - step if side == 0 else zpos + step

    def present(side, step):
        return zpos >= step if side == 0 else zpos + step < zsize

    def forward_filter(step, chunk):
        for side in range(2):

            @pl.when(present(side, step))
            def _(side=side):
                block = origin(side, step) * 2 + ypos
                source = filter_block(block, chunk)
                zfil_copy(side, step - 1, own_filter(chunk), block, chunk).wait_recv()
                yfil_copy(side, step, source, block, chunk).start()

                @pl.when(has_next[side])
                def _():
                    zfil_copy(side, step, source, block, chunk).start()

    direct = [i for i, offset in enumerate(offsets) if offset[1] == 0 or offset[0] == 0]
    relayed = [i for i in range(len(offsets)) if i not in direct]
    for i in direct:
        taps_copy(i, taps_ref, me).start()
    for chunk in range(chunks):
        yfil_copy(0, 0, own_filter(chunk), dp, chunk).start()
        for side in range(2):

            @pl.when(has_next[side])
            def _(side=side, chunk=chunk):
                zfil_copy(side, 0, own_filter(chunk), dp, chunk).start()

    x_copy.wait()
    halo_out[...] = x_ref[:, rows - (kernel_size - 1) :, :]
    halo_copy = pltpu.make_async_remote_copy(
        src_ref=halo_out,
        dst_ref=halo_in,
        send_sem=halo_send,
        recv_sem=halo_recv,
        device_id={"ctx": following},
        device_id_type=MESH,
    )
    halo_copy.start()
    own_taps_copy.wait()
    for i in direct:
        taps_copy(i, taps_ref, sources[i]).wait_recv()
    for i in relayed:
        taps_copy(i, taps_all.at[sources[i - 1]], sources[i - 1]).start()
    halo_copy.wait_recv()

    row_index = lax.broadcasted_iota(jnp.int32, (rows, CHUNK), 0)

    def short_filter(stream, owner, chunk):
        columns = pl.ds(pl.multiple_of(owner * channels + chunk * CHUNK, CHUNK), CHUNK)
        taps_columns = pl.ds(pl.multiple_of(chunk * CHUNK, CHUNK), CHUNK)
        values = x_ref[stream, :, columns].astype(jnp.float32)
        edge = halo_in[stream, :, columns].astype(jnp.float32)
        edge = jnp.where(me > 0, edge, jnp.zeros_like(edge))
        total = taps_all[owner, 0, stream : stream + 1, taps_columns] * values
        for tap in range(1, kernel_size):
            moved = pltpu.roll(values, tap, 0)
            for row in range(tap):
                at = kernel_size - 1 + row - tap
                moved = jnp.where(row_index == row, edge[at : at + 1], moved)
            total = total + taps_all[owner, tap, stream : stream + 1, taps_columns] * moved
        return total

    def gated_rows(owner, chunk):
        return (short_filter(1, owner, chunk) * short_filter(2, owner, chunk)).astype(jnp.bfloat16)

    def position_rows(owner):
        return pl.ds(pl.multiple_of(owner * rows, rows), rows)

    def gated_copy(i, chunk, owner):
        return pltpu.make_async_remote_copy(
            src_ref=gated_out.at[i, chunk],
            dst_ref=gated_slab.at[chunk, position_rows(owner), :],
            send_sem=gated_send.at[i, chunk],
            recv_sem=gated_recv.at[i, chunk],
            device_id={"ctx": dests[i]},
            device_id_type=MESH,
        )

    def response_copy(i, chunk):
        return pltpu.make_async_remote_copy(
            src_ref=response_slab.at[chunk, position_rows(dests[i]), :],
            dst_ref=response_in.at[i, chunk],
            send_sem=resp_send.at[i, chunk],
            recv_sem=resp_recv.at[i, chunk],
            device_id={"ctx": dests[i]},
            device_id_type=MESH,
        )

    def push_gated(i, chunk):
        gated_out[i, chunk] = gated_rows(dests[i], chunk)
        gated_copy(i, chunk, me).start()

    for i in direct:
        push_gated(i, 0)
    for i in relayed:
        taps_copy(i, taps_ref, sources[i]).wait_recv()
        push_gated(i, 0)
    gated_slab[0, position_rows(me), :] = gated_rows(me, 0)

    forward_filter(1, 0)

    def push_chunk(chunk, carry):
        for i in range(len(offsets)):
            push_gated(i, chunk)
        forward_filter(1, chunk)
        gated_slab[chunk, position_rows(me), :] = gated_rows(me, chunk)
        return carry

    lax.fori_loop(1, chunks, push_chunk, 0)

    def fill_queries(chunk, carry):
        forward_filter(2, chunk)

        def one_owner(owner, inner):
            queries[owner, chunk] = short_filter(0, owner, chunk).astype(jnp.bfloat16)
            return inner

        return lax.fori_loop(0, ctx_size, one_owner, carry)

    lax.fori_loop(0, chunks, fill_queries, 0)
    for step in range(3, zsize):
        lax.fori_loop(0, chunks, lambda chunk, _: forward_filter(step, chunk) or 0, 0)
    forward_copy.wait()
    backward_copy.wait()
    skip_copy.wait()

    def convolve(chunk, carry):
        columns = pl.ds(pl.multiple_of(chunk * CHUNK, CHUNK), CHUNK)
        own_filter_copy(chunk).wait()
        yfil_copy(0, 0, own_filter(chunk), ypeer, chunk).wait_recv()
        for side in range(2):
            for step in range(1, zsize):

                @pl.when(present(side, step))
                def _(side=side, step=step):
                    block = origin(side, step) * 2 + 1 - ypos
                    yfil_copy(side, step, own_filter(chunk), block, chunk).wait_recv()

        filter_spec[...] = jnp.dot(
            forward_ref[...], filter_slab[chunk], preferred_element_type=jnp.float32
        )
        for i in range(len(offsets)):
            gated_copy(i, chunk, sources[i]).wait_recv()
        gated = gated_slab[chunk]
        sig_cos = jnp.dot(forward_ref[:length], gated, preferred_element_type=jnp.float32)
        sig_sin = jnp.dot(forward_ref[length:], gated, preferred_element_type=jnp.float32)
        ker_cos, ker_sin = filter_spec[:length], filter_spec[length:]
        prod_ref[:length] = (sig_cos * ker_cos - sig_sin * ker_sin).astype(jnp.bfloat16)
        prod_ref[length:] = (sig_cos * ker_sin + sig_sin * ker_cos).astype(jnp.bfloat16)
        long_part = jnp.dot(backward_ref[...], prod_ref[...], preferred_element_type=jnp.float32)
        direct = skip_ref[:, columns] * gated.astype(jnp.float32)
        response_slab[chunk] = (long_part + direct).astype(jnp.bfloat16)
        for i in range(len(offsets)):
            response_copy(i, chunk).start()
        mix_into(me, chunk, response_slab[chunk, position_rows(me), :])
        return carry

    def out_copy(owner, chunk):
        columns = pl.ds(pl.multiple_of(owner * channels + chunk * CHUNK, CHUNK), CHUNK)
        return pltpu.make_async_copy(
            queries.at[owner, chunk], out_hbm.at[:, columns], out_sem.at[owner, chunk]
        )

    def mix_into(owner, chunk, response):
        mixed = queries[owner, chunk].astype(jnp.float32) * response.astype(jnp.float32)
        queries[owner, chunk] = mixed.astype(jnp.bfloat16)
        out_copy(owner, chunk).start()

    lax.fori_loop(0, chunks, convolve, 0)

    def finish(chunk, carry):
        for i in reversed(range(len(offsets))):
            response_copy(i, chunk).wait_recv()
            mix_into(sources[i], chunk, response_in[i, chunk])
        return carry

    lax.fori_loop(0, chunks, finish, 0)

    def drain(chunk, carry):
        for i in range(len(offsets)):
            gated_copy(i, chunk, me).wait_send()
            response_copy(i, chunk).wait_send()
        for owner in range(ctx_size):
            out_copy(owner, chunk).wait()
        yfil_copy(0, 0, own_filter(chunk), dp, chunk).wait_send()
        for side in range(2):

            @pl.when(has_next[side])
            def _(side=side):
                zfil_copy(side, 0, own_filter(chunk), dp, chunk).wait_send()

            for step in range(1, zsize):

                @pl.when(present(side, step))
                def _(side=side, step=step):
                    block = origin(side, step) * 2 + ypos
                    source = filter_block(block, chunk)
                    yfil_copy(side, step, source, block, chunk).wait_send()

                    @pl.when(has_next[side])
                    def _():
                        zfil_copy(side, step, source, block, chunk).wait_send()

        return carry

    lax.fori_loop(0, chunks, drain, 0)
    for i in range(len(offsets)):
        taps_copy(i, taps_ref, me).wait_send()
    halo_copy.wait_send()


def on_device(projected, short_taps, long_filter, skip_gain):
    ctx_size, dp_size = lax.axis_size("ctx"), lax.axis_size("dp")
    kernel_size, streams, channels = short_taps.shape
    rows, width = projected.shape[1], projected.shape[3]
    length = rows * ctx_size
    regular = ctx_size % 2 == 0 and dp_size % 2 == 0 and dp_size >= 6 and channels % CHUNK == 0
    if length > 1024 or not regular:
        return on_device_large(projected, short_taps, long_filter, skip_gain)
    forward, backward = quarter_tables(length)
    chunks = channels // CHUNK
    peers = ctx_size - 1
    zsize = dp_size // 2
    hbm_spec = pl.BlockSpec(memory_space=pltpu.HBM)
    dma = pltpu.SemaphoreType.DMA
    mixed = pl.pallas_call(
        functools.partial(mixer_kernel, ctx_size, dp_size),
        out_shape=jax.ShapeDtypeStruct((rows, width), jnp.bfloat16),
        in_specs=[hbm_spec] * 6,
        out_specs=hbm_spec,
        scratch_shapes=[
            pltpu.VMEM((streams, rows, width), jnp.bfloat16),
            pltpu.VMEM((1, channels), jnp.float32),
            pltpu.VMEM(forward.shape, jnp.bfloat16),
            pltpu.VMEM(backward.shape, jnp.bfloat16),
            pltpu.VMEM((ctx_size, kernel_size, streams, channels), jnp.float32),
            pltpu.VMEM((streams, kernel_size - 1, width), jnp.bfloat16),
            pltpu.VMEM((streams, kernel_size - 1, width), jnp.bfloat16),
            pltpu.VMEM((peers, chunks, rows, CHUNK), jnp.bfloat16),
            pltpu.VMEM((chunks, length, CHUNK), jnp.bfloat16),
            pltpu.VMEM((chunks, length, CHUNK), jnp.bfloat16),
            pltpu.VMEM((2 * length, CHUNK), jnp.float32),
            pltpu.VMEM((2 * length, CHUNK), jnp.bfloat16),
            pltpu.VMEM((chunks, length, CHUNK), jnp.bfloat16),
            pltpu.VMEM((peers, chunks, rows, CHUNK), jnp.bfloat16),
            pltpu.VMEM((ctx_size, chunks, rows, CHUNK), jnp.bfloat16),
            dma((5,)),
            dma((peers,)),
            dma((peers,)),
            dma,
            dma,
            dma((2, zsize, chunks)),
            dma((2, zsize, chunks)),
            dma((2, zsize, chunks)),
            dma((2, zsize, chunks)),
            dma((peers, chunks)),
            dma((peers, chunks)),
            dma((peers, chunks)),
            dma((peers, chunks)),
            dma((ctx_size, chunks)),
            dma((chunks,)),
        ],
        compiler_params=pltpu.CompilerParams(
            collective_id=0, has_side_effects=True, vmem_limit_bytes=62 * 2**20
        ),
    )(
        projected[0].transpose(1, 0, 2),
        short_taps,
        long_filter,
        skip_gain[None],
        forward,
        backward,
    )
    return mixed[None]


def solution(mesh):
    return jax.shard_map(
        on_device,
        mesh=mesh,
        in_specs=(P("dp", "ctx", None, None), P(None, None, "ctx"), P("dp", "ctx"), P("ctx")),
        out_specs=P("dp", "ctx", None),
        check_vma=False,
    )
```

```python
import functools
import math

import jax
import jax.numpy as jnp
import numpy as np
from jax import lax
from jax.experimental import pallas as pl
from jax.experimental.pallas import tpu as pltpu
from jax.sharding import PartitionSpec as P

RADIX = 64


HIGH = lax.Precision.HIGHEST


def causal_short(extended, taps, kernel_size):
    row_count = extended.shape[0] - (kernel_size - 1)
    widened = extended.astype(jnp.float32)
    summed = jnp.zeros((row_count,) + widened.shape[1:], jnp.float32)
    for tap_index in range(kernel_size):
        offset = kernel_size - 1 - tap_index
        summed = summed + taps[tap_index] * widened[offset : offset + row_count]
    return (summed[:, 0].astype(jnp.bfloat16), (summed[:, 1] * summed[:, 2]).astype(jnp.bfloat16))


def dft_tables(length, radix_size):
    outer_size = 2 * length // radix_size
    total_size = outer_size * radix_size
    outer_range = jnp.arange(outer_size, dtype=jnp.int32)
    inner_range = jnp.arange(radix_size, dtype=jnp.int32)
    angle_one = (
        2.0
        * math.pi
        / outer_size
        * (outer_range[:, None] * outer_range[None, :] % outer_size).astype(jnp.float32)
    )
    angle_twist = (
        2.0
        * math.pi
        / total_size
        * (outer_range[:, None] * inner_range[None, :] % total_size).astype(jnp.float32)
    )
    angle_two = (
        2.0
        * math.pi
        / radix_size
        * (inner_range[:, None] * inner_range[None, :] % radix_size).astype(jnp.float32)
    )
    twist_cos = jnp.cos(angle_twist)[:, :, None]
    twist_sin = jnp.sin(angle_twist)[:, :, None]
    return (
        jnp.cos(angle_one),
        jnp.sin(angle_one),
        twist_cos,
        twist_sin,
        jnp.cos(angle_two),
        jnp.sin(angle_two),
    )


def forward_dft(signal, tables, radix_size):
    cos_one, sin_one, twist_cos, twist_sin, cos_two, sin_two = tables
    outer_size = cos_one.shape[0]
    half_size = outer_size // 2
    block_width = signal.shape[1]
    shaped = signal.reshape(half_size, radix_size * block_width)
    first_re = jnp.dot(cos_one[:, :half_size], shaped, precision=HIGH).reshape(
        outer_size, radix_size, block_width
    )
    first_im = -jnp.dot(sin_one[:, :half_size], shaped, precision=HIGH).reshape(
        outer_size, radix_size, block_width
    )
    second_re = first_re * twist_cos + first_im * twist_sin
    second_im = first_im * twist_cos - first_re * twist_sin
    spec_re = jnp.einsum("amc,mb->abc", second_re, cos_two, precision=HIGH) + jnp.einsum(
        "amc,mb->abc", second_im, sin_two, precision=HIGH
    )
    spec_im = jnp.einsum("amc,mb->abc", second_im, cos_two, precision=HIGH) - jnp.einsum(
        "amc,mb->abc", second_re, sin_two, precision=HIGH
    )
    return (spec_re, spec_im)


def inverse_dft(spec_re, spec_im, tables, radix_size):
    cos_one, sin_one, twist_cos, twist_sin, cos_two, sin_two = tables
    outer_size = cos_one.shape[0]
    half_size = outer_size // 2
    block_width = spec_re.shape[2]
    back_re = jnp.einsum("abc,mb->amc", spec_re, cos_two, precision=HIGH) - jnp.einsum(
        "abc,mb->amc", spec_im, sin_two, precision=HIGH
    )
    back_im = jnp.einsum("abc,mb->amc", spec_re, sin_two, precision=HIGH) + jnp.einsum(
        "abc,mb->amc", spec_im, cos_two, precision=HIGH
    )
    turned_re = (back_re * twist_cos - back_im * twist_sin).reshape(
        outer_size, radix_size * block_width
    )
    turned_im = (back_re * twist_sin + back_im * twist_cos).reshape(
        outer_size, radix_size * block_width
    )
    result = jnp.dot(cos_one[:half_size], turned_re, precision=HIGH) - jnp.dot(
        sin_one[:half_size], turned_im, precision=HIGH
    )
    return result.reshape(half_size * radix_size, block_width) / (outer_size * radix_size)


def long_convolve_blocked(gated_slab, filter_slab):
    length, channels = gated_slab.shape
    block_width = min(128, channels)
    tables = dft_tables(length, RADIX)

    def one_block(block_index, output):
        offset = block_index * block_width
        signal = lax.dynamic_slice_in_dim(gated_slab, offset, block_width, 1).astype(jnp.float32)
        kernel_block = lax.dynamic_slice_in_dim(filter_slab, offset, block_width, 1).astype(
            jnp.float32
        )
        sig_re, sig_im = forward_dft(signal, tables, RADIX)
        ker_re, ker_im = forward_dft(kernel_block, tables, RADIX)
        prod_re = sig_re * ker_re - sig_im * ker_im
        prod_im = sig_re * ker_im + sig_im * ker_re
        result = inverse_dft(prod_re, prod_im, tables, RADIX)
        return lax.dynamic_update_slice_in_dim(output, result, offset, 1)

    return lax.fori_loop(
        0, channels // block_width, one_block, jnp.zeros((length, channels), jnp.float32)
    )


def long_convolve(gated_slab, filter_slab):
    length = gated_slab.shape[0]
    if length > 1024:
        return long_convolve_blocked(gated_slab, filter_slab)
    forward, backward = quarter_tables(length)
    sig = jnp.dot(forward, gated_slab, preferred_element_type=jnp.float32)
    ker = jnp.dot(forward, filter_slab, preferred_element_type=jnp.float32)
    sig_cos, sig_sin, ker_cos, ker_sin = sig[:length], sig[length:], ker[:length], ker[length:]
    prod = jnp.concatenate(
        [sig_cos * ker_cos - sig_sin * ker_sin, sig_cos * ker_sin + sig_sin * ker_cos]
    ).astype(jnp.bfloat16)
    return jnp.dot(backward, prod, preferred_element_type=jnp.float32)


def quarter_tables(length):
    steps = (4 * np.arange(length)[:, None] + 1) * np.arange(length)[None, :] % (4 * length)
    angles = steps * (2.0 * math.pi / (4 * length))
    table = np.concatenate([np.cos(angles), np.sin(angles)])
    return (jnp.asarray(table, jnp.bfloat16), jnp.asarray(table.T / length, jnp.bfloat16))


def make_response(gated_slab, filter_slab, skip_gain):
    long_part = long_convolve(gated_slab, filter_slab)
    return (long_part + skip_gain * gated_slab.astype(jnp.float32)).astype(jnp.bfloat16)


def combine_rows(query_part, response_part):
    return (query_part.astype(jnp.float32) * response_part.astype(jnp.float32)).astype(jnp.bfloat16)


def on_device_large(projected, short_taps, long_filter, skip_gain):
    kernel_size = short_taps.shape[0]
    ctx_size = lax.axis_size("ctx")
    rows = projected[0]
    filter_slab = lax.all_gather(long_filter, "dp", axis=0, tiled=True)
    all_taps = lax.all_gather(short_taps, "ctx", axis=2, tiled=True)
    halo = lax.ppermute(
        rows[-(kernel_size - 1) :], "ctx", [(i, i + 1) for i in range(ctx_size - 1)]
    )
    queries, gated = causal_short(jnp.concatenate([halo, rows]), all_taps, kernel_size)
    gated_slab = lax.all_to_all(gated, "ctx", split_axis=1, concat_axis=0, tiled=True)
    response_slab = make_response(gated_slab, filter_slab, skip_gain)
    response = lax.all_to_all(response_slab, "ctx", split_axis=0, concat_axis=1, tiled=True)
    return combine_rows(queries, response)[None]


CHUNK = 256
MESH = pl.DeviceIdType.MESH


def ctx_offsets(ctx_size):
    pairs = [(a, b) for a in range(1, ctx_size // 2) for b in range(2)]
    return pairs + [(0, 1)]


def ctx_peer(me, offset, ctx_size, sign):
    half = ctx_size // 2
    chip = lax.rem(me // 2 + (half + sign * offset[0]) % half, half)
    core = lax.rem(lax.rem(me, 2) + offset[1], 2)
    return chip * 2 + core


def mixer_kernel(
    ctx_size,
    dp_size,
    x_hbm,
    taps_ref,
    filter_ref,
    skip_hbm,
    forward_hbm,
    backward_hbm,
    queries_hbm,
    response_hbm,
    x_ref,
    skip_ref,
    forward_ref,
    backward_ref,
    taps_all,
    halo_out,
    halo_in,
    gated_out,
    gated_slab,
    filter_slab,
    filter_spec,
    prod_ref,
    response_slab,
    queries,
    local_sem,
    taps_send,
    taps_recv,
    halo_send,
    halo_recv,
    zfil_send,
    zfil_recv,
    yfil_send,
    yfil_recv,
    gated_send,
    gated_recv,
    resp_send,
    resp_recv,
    out_sem,
    filter_sem,
    response_sem,
):
    kernel_size = taps_ref.shape[0]
    channels = taps_ref.shape[2]
    rows = x_ref.shape[1]
    length = rows * ctx_size
    chunks = channels // CHUNK
    fil_rows = filter_ref.shape[0]
    zsize = dp_size // 2
    me = lax.axis_index("ctx")
    dp = lax.axis_index("dp")
    zpos, ypos = dp // 2, lax.rem(dp, 2)
    offsets = ctx_offsets(ctx_size)
    dests = [ctx_peer(me, o, ctx_size, 1) for o in offsets]
    sources = [ctx_peer(me, o, ctx_size, -1) for o in offsets]
    following = lax.rem(me + 1, ctx_size)
    ypeer = zpos * 2 + (1 - ypos)

    def filter_block(block, chunk):
        return filter_slab.at[
            chunk, pl.ds(pl.multiple_of(block * fil_rows, fil_rows), fil_rows), :
        ]

    def own_filter(chunk):
        return filter_ref.at[:, pl.ds(pl.multiple_of(chunk * CHUNK, CHUNK), CHUNK)]

    def own_filter_copy(chunk):
        return pltpu.make_async_copy(
            own_filter(chunk), filter_block(dp, chunk), filter_sem.at[chunk]
        )

    x_copy = pltpu.make_async_copy(x_hbm, x_ref, local_sem.at[0])
    x_copy.start()
    forward_copy = pltpu.make_async_copy(forward_hbm, forward_ref, local_sem.at[1])
    forward_copy.start()
    backward_copy = pltpu.make_async_copy(backward_hbm, backward_ref, local_sem.at[2])
    backward_copy.start()
    skip_copy = pltpu.make_async_copy(skip_hbm, skip_ref, local_sem.at[3])
    skip_copy.start()
    own_taps_copy = pltpu.make_async_copy(taps_ref, taps_all.at[me], local_sem.at[4])
    own_taps_copy.start()
    for chunk in range(chunks):
        own_filter_copy(chunk).start()

    barrier = pltpu.get_barrier_semaphore()
    for dest in dests:
        pl.semaphore_signal(barrier, inc=1, device_id={"ctx": dest}, device_id_type=MESH)
    pl.semaphore_signal(barrier, inc=1, device_id={"dp": ypeer}, device_id_type=MESH)

    for turn in (1, zsize - 1):
        side_peer = lax.rem(zpos + turn, zsize) * 2 + ypos
        pl.semaphore_signal(barrier, inc=1, device_id={"dp": side_peer}, device_id_type=MESH)
    pl.semaphore_wait(barrier, len(dests) + 3)

    def taps_copy(i, source, slot):
        return pltpu.make_async_remote_copy(
            src_ref=source,
            dst_ref=taps_all.at[slot],
            send_sem=taps_send.at[i],
            recv_sem=taps_recv.at[i],
            device_id={"ctx": dests[i] if offsets[i][1] == 0 else dests[-1]},
            device_id_type=MESH,
        )

    def zfil_copy(side, step, source, block, chunk):
        return pltpu.make_async_remote_copy(
            src_ref=source,
            dst_ref=filter_block(block, chunk),
            send_sem=zfil_send.at[side, step, chunk],
            recv_sem=zfil_recv.at[side, step, chunk],
            device_id={"dp": dp + 2 - 4 * side},
            device_id_type=MESH,
        )

    def yfil_copy(side, step, source, block, chunk):
        return pltpu.make_async_remote_copy(
            src_ref=source,
            dst_ref=filter_block(block, chunk),
            send_sem=yfil_send.at[side, step, chunk],
            recv_sem=yfil_recv.at[side, step, chunk],
            device_id={"dp": ypeer},
            device_id_type=MESH,
        )

    has_next = (zpos < zsize - 1, zpos > 0)

    def origin(side, step):
        return zpos - step if side == 0 else zpos + step

    def present(side, step):
        return zpos >= step if side == 0 else zpos + step < zsize

    def forward_filter(step, chunk):
        for side in range(2):

            @pl.when(present(side, step))
            def _(side=side):
                block = origin(side, step) * 2 + ypos
                source = filter_block(block, chunk)
                zfil_copy(side, step - 1, own_filter(chunk), block, chunk).wait_recv()
                yfil_copy(side, step, source, block, chunk).start()

                @pl.when(has_next[side])
                def _():
                    zfil_copy(side, step, source, block, chunk).start()

    direct = [i for i, offset in enumerate(offsets) if offset[1] == 0 or offset[0] == 0]
    relayed = [i for i in range(len(offsets)) if i not in direct]
    for i in direct:
        taps_copy(i, taps_ref, me).start()
    for chunk in range(chunks):
        yfil_copy(0, 0, own_filter(chunk), dp, chunk).start()
        for side in range(2):

            @pl.when(has_next[side])
            def _(side=side, chunk=chunk):
                zfil_copy(side, 0, own_filter(chunk), dp, chunk).start()

    x_copy.wait()
    halo_out[...] = x_ref[:, rows - (kernel_size - 1) :, :]
    halo_copy = pltpu.make_async_remote_copy(
        src_ref=halo_out,
        dst_ref=halo_in,
        send_sem=halo_send,
        recv_sem=halo_recv,
        device_id={"ctx": following},
        device_id_type=MESH,
    )
    halo_copy.start()
    own_taps_copy.wait()
    for i in direct:
        taps_copy(i, taps_ref, sources[i]).wait_recv()
    for i in relayed:
        taps_copy(i, taps_all.at[sources[i - 1]], sources[i - 1]).start()
    halo_copy.wait_recv()

    row_index = lax.broadcasted_iota(jnp.int32, (rows, CHUNK), 0)

    def short_filter(stream, owner, chunk):
        columns = pl.ds(pl.multiple_of(owner * channels + chunk * CHUNK, CHUNK), CHUNK)
        taps_columns = pl.ds(pl.multiple_of(chunk * CHUNK, CHUNK), CHUNK)
        values = x_ref[stream, :, columns].astype(jnp.float32)
        edge = halo_in[stream, :, columns].astype(jnp.float32)
        edge = jnp.where(me > 0, edge, jnp.zeros_like(edge))
        total = taps_all[owner, 0, stream : stream + 1, taps_columns] * values
        for tap in range(1, kernel_size):
            moved = pltpu.roll(values, tap, 0)
            for row in range(tap):
                at = kernel_size - 1 + row - tap
                moved = jnp.where(row_index == row, edge[at : at + 1], moved)
            total = total + taps_all[owner, tap, stream : stream + 1, taps_columns] * moved
        return total

    def gated_rows(owner, chunk):
        return (short_filter(1, owner, chunk) * short_filter(2, owner, chunk)).astype(jnp.bfloat16)

    def position_rows(owner):
        return pl.ds(pl.multiple_of(owner * rows, rows), rows)

    def gated_copy(i, chunk, owner):
        return pltpu.make_async_remote_copy(
            src_ref=gated_out.at[i, chunk],
            dst_ref=gated_slab.at[chunk, position_rows(owner), :],
            send_sem=gated_send.at[i, chunk],
            recv_sem=gated_recv.at[i, chunk],
            device_id={"ctx": dests[i]},
            device_id_type=MESH,
        )

    def columns_of(owner, chunk):
        return pl.ds(pl.multiple_of(owner * channels + chunk * CHUNK, CHUNK), CHUNK)

    def response_copy(i, chunk, owner):
        return pltpu.make_async_remote_copy(
            src_ref=response_slab.at[chunk, position_rows(dests[i]), :],
            dst_ref=response_hbm.at[:, columns_of(owner, chunk)],
            send_sem=resp_send.at[i, chunk],
            recv_sem=resp_recv.at[i, chunk],
            device_id={"ctx": dests[i]},
            device_id_type=MESH,
        )

    def push_gated(i, chunk):
        gated_out[i, chunk] = gated_rows(dests[i], chunk)
        gated_copy(i, chunk, me).start()

    for i in direct:
        push_gated(i, 0)
    for i in relayed:
        taps_copy(i, taps_ref, sources[i]).wait_recv()
        push_gated(i, 0)
    gated_slab[0, position_rows(me), :] = gated_rows(me, 0)

    forward_filter(1, 0)

    def push_chunk(chunk, carry):
        for i in range(len(offsets)):
            push_gated(i, chunk)
        forward_filter(1, chunk)
        gated_slab[chunk, position_rows(me), :] = gated_rows(me, chunk)
        return carry

    lax.fori_loop(1, chunks, push_chunk, 0)

    def out_copy(owner, chunk):
        return pltpu.make_async_copy(
            queries.at[owner, chunk],
            queries_hbm.at[:, columns_of(owner, chunk)],
            out_sem.at[owner, chunk],
        )

    def fill_queries(chunk, carry):
        forward_filter(2, chunk)

        def one_owner(owner, inner):
            queries[owner, chunk] = short_filter(0, owner, chunk).astype(jnp.bfloat16)
            out_copy(owner, chunk).start()
            return inner

        return lax.fori_loop(0, ctx_size, one_owner, carry)

    lax.fori_loop(0, chunks, fill_queries, 0)
    for step in range(3, zsize):
        lax.fori_loop(0, chunks, lambda chunk, _: forward_filter(step, chunk) or 0, 0)
    forward_copy.wait()
    backward_copy.wait()
    skip_copy.wait()

    def convolve(chunk, carry):
        columns = pl.ds(pl.multiple_of(chunk * CHUNK, CHUNK), CHUNK)
        own_filter_copy(chunk).wait()
        yfil_copy(0, 0, own_filter(chunk), ypeer, chunk).wait_recv()
        for side in range(2):
            for step in range(1, zsize):

                @pl.when(present(side, step))
                def _(side=side, step=step):
                    block = origin(side, step) * 2 + 1 - ypos
                    yfil_copy(side, step, own_filter(chunk), block, chunk).wait_recv()

        filter_spec[...] = jnp.dot(
            forward_ref[...], filter_slab[chunk], preferred_element_type=jnp.float32
        )
        for i in range(len(offsets)):
            gated_copy(i, chunk, sources[i]).wait_recv()
        gated = gated_slab[chunk]
        sig_cos = jnp.dot(forward_ref[:length], gated, preferred_element_type=jnp.float32)
        sig_sin = jnp.dot(forward_ref[length:], gated, preferred_element_type=jnp.float32)
        ker_cos, ker_sin = filter_spec[:length], filter_spec[length:]
        prod_ref[:length] = (sig_cos * ker_cos - sig_sin * ker_sin).astype(jnp.bfloat16)
        prod_ref[length:] = (sig_cos * ker_sin + sig_sin * ker_cos).astype(jnp.bfloat16)
        long_part = jnp.dot(backward_ref[...], prod_ref[...], preferred_element_type=jnp.float32)
        direct = skip_ref[:, columns] * gated.astype(jnp.float32)
        response_slab[chunk] = (long_part + direct).astype(jnp.bfloat16)
        for i in range(len(offsets)):
            response_copy(i, chunk, me).start()
        own_response(chunk).start()
        return carry

    def own_response(chunk):
        return pltpu.make_async_copy(
            response_slab.at[chunk, position_rows(me), :],
            response_hbm.at[:, columns_of(me, chunk)],
            response_sem.at[chunk],
        )

    lax.fori_loop(0, chunks, convolve, 0)

    def finish(chunk, carry):
        for i in reversed(range(len(offsets))):
            response_copy(i, chunk, sources[i]).wait_recv()
        return carry

    lax.fori_loop(0, chunks, finish, 0)

    def drain(chunk, carry):
        for i in range(len(offsets)):
            gated_copy(i, chunk, me).wait_send()
            response_copy(i, chunk, me).wait_send()
        own_response(chunk).wait()
        for owner in range(ctx_size):
            out_copy(owner, chunk).wait()
        yfil_copy(0, 0, own_filter(chunk), dp, chunk).wait_send()
        for side in range(2):

            @pl.when(has_next[side])
            def _(side=side):
                zfil_copy(side, 0, own_filter(chunk), dp, chunk).wait_send()

            for step in range(1, zsize):

                @pl.when(present(side, step))
                def _(side=side, step=step):
                    block = origin(side, step) * 2 + ypos
                    source = filter_block(block, chunk)
                    yfil_copy(side, step, source, block, chunk).wait_send()

                    @pl.when(has_next[side])
                    def _():
                        zfil_copy(side, step, source, block, chunk).wait_send()

        return carry

    lax.fori_loop(0, chunks, drain, 0)
    for i in range(len(offsets)):
        taps_copy(i, taps_ref, me).wait_send()
    halo_copy.wait_send()


def on_device(projected, short_taps, long_filter, skip_gain):
    ctx_size, dp_size = lax.axis_size("ctx"), lax.axis_size("dp")
    kernel_size, streams, channels = short_taps.shape
    rows, width = projected.shape[1], projected.shape[3]
    length = rows * ctx_size
    regular = ctx_size % 2 == 0 and dp_size % 2 == 0 and dp_size >= 6 and channels % CHUNK == 0
    if length > 1024 or not regular:
        return on_device_large(projected, short_taps, long_filter, skip_gain)
    forward, backward = quarter_tables(length)
    chunks = channels // CHUNK
    peers = ctx_size - 1
    zsize = dp_size // 2
    hbm_spec = pl.BlockSpec(memory_space=pltpu.HBM)
    dma = pltpu.SemaphoreType.DMA
    queries, response = pl.pallas_call(
        functools.partial(mixer_kernel, ctx_size, dp_size),
        out_shape=[jax.ShapeDtypeStruct((rows, width), jnp.bfloat16)] * 2,
        in_specs=[hbm_spec] * 6,
        out_specs=[hbm_spec] * 2,
        scratch_shapes=[
            pltpu.VMEM((streams, rows, width), jnp.bfloat16),
            pltpu.VMEM((1, channels), jnp.float32),
            pltpu.VMEM(forward.shape, jnp.bfloat16),
            pltpu.VMEM(backward.shape, jnp.bfloat16),
            pltpu.VMEM((ctx_size, kernel_size, streams, channels), jnp.float32),
            pltpu.VMEM((streams, kernel_size - 1, width), jnp.bfloat16),
            pltpu.VMEM((streams, kernel_size - 1, width), jnp.bfloat16),
            pltpu.VMEM((peers, chunks, rows, CHUNK), jnp.bfloat16),
            pltpu.VMEM((chunks, length, CHUNK), jnp.bfloat16),
            pltpu.VMEM((chunks, length, CHUNK), jnp.bfloat16),
            pltpu.VMEM((2 * length, CHUNK), jnp.float32),
            pltpu.VMEM((2 * length, CHUNK), jnp.bfloat16),
            pltpu.VMEM((chunks, length, CHUNK), jnp.bfloat16),
            pltpu.VMEM((ctx_size, chunks, rows, CHUNK), jnp.bfloat16),
            dma((5,)),
            dma((peers,)),
            dma((peers,)),
            dma,
            dma,
            dma((2, zsize, chunks)),
            dma((2, zsize, chunks)),
            dma((2, zsize, chunks)),
            dma((2, zsize, chunks)),
            dma((peers, chunks)),
            dma((peers, chunks)),
            dma((peers, chunks)),
            dma((peers, chunks)),
            dma((ctx_size, chunks)),
            dma((chunks,)),
            dma((chunks,)),
        ],
        compiler_params=pltpu.CompilerParams(
            collective_id=0, has_side_effects=True, vmem_limit_bytes=62 * 2**20
        ),
    )(
        projected[0].transpose(1, 0, 2),
        short_taps,
        long_filter,
        skip_gain[None],
        forward,
        backward,
    )
    return combine_rows(queries, response)[None]


def solution(mesh):
    return jax.shard_map(
        on_device,
        mesh=mesh,
        in_specs=(P("dp", "ctx", None, None), P(None, None, "ctx"), P("dp", "ctx"), P("ctx")),
        out_specs=P("dp", "ctx", None),
        check_vma=False,
    )
```
